256 devices in a mesh: tm: 8 (over x, y_hi), space: 32 (over y_lo, z, core).
Axes of the slice: x: 4, y: 4 (y_hi: 2, y_lo: 2; y = y_hi * 2 + y_lo), z: 8, core: 2. Of those that a mesh axis runs over, the one named last changes fastest.
Arguments:
- slice_starts: float32 [8, 64, 32768], P('tm', None, 'space'), may hold values from -3 to 3
- window_entry: float32 [64, 32768], P(None, 'space'), may hold values from -3 to 3
- cell_order: int32 [32, 1024], P('space'), may hold values from 0 to 1023, each once within a row
- coarse_counts: int32 [8], P('tm'), may hold values from 1 to 4
- advection_matrix: float32 [64, 64], replicated, may hold values from -0.75 to 0.75
- viscous_matrix: float32 [64, 64], replicated, may hold values from -0.75 to 0.75
- lift_matrix: float32 [64, 96], replicated, may hold values from -0.625 to 0.625
Outputs:
- next_starts: float32 [8, 64, 32768], P('tm', None, 'space')
- next_interiors: float32 [8, 64, 32768], P('tm', None, 'space')
The draws below stay inside these ranges and needn't reach their ends.
Inputs may be any that keep to these rules, and one draw needn't show every extreme that they name: `cell_order`: each row lists every cell of one partition's block exactly once.
All inputs are finite; a program needn't handle non-finite values.
Results may differ from the reference program's by a relative error of at most 0.0003.
Values sent between devices are 32-bit elements; how exact they have to be, the bound alone decides.
A program may use at most 64 MiB of HBM per device.

```python
import jax
import jax.numpy as jnp
from jax import lax

NODES = 4
DOFS = 64
FACE_DOFS = 16
LY = 32
LZ = 32
STEPS = 2
E_DEV = 1024
PARTS_SIZE = 32
ELEMS = 32768
SLICES = 8


def plant(values, stream_key, smallest, top_value):
    dims = values.shape
    index_at = [jax.random.randint(jax.random.fold_in(stream_key, axis), (), 0, dims[axis]) for axis in range(len(dims))]
    values = values.at[tuple(index_at)].set(smallest)
    longest = dims.index(max(dims))
    index_at[longest] = (index_at[longest] + 1) % dims[longest]
    return values.at[tuple(index_at)].set(top_value)


def block_levels(key, shape, shards, smallest, top_value):
    def one(position, shards_of):
        draws = jax.random.uniform(jax.random.fold_in(jax.random.fold_in(key, 6), position), (shards_of,), jnp.float32, smallest / len(shards), top_value / len(shards))
        return jnp.repeat(jnp.exp(draws), shape[position] // shards_of).reshape((-1,) + (1,) * (len(shape) - position - 1))

    level = one(*shards[0])
    for cut in shards[1:]:
        level = level * one(*cut)
    return level


def normal_values(own_key, extent, scale, reach, pieces=(), held_as=jnp.bfloat16):
    drawn = scale * jax.random.normal(own_key, extent, jnp.float32)
    if pieces:
        drawn = drawn * block_levels(own_key, extent, pieces, -0.22, 0.18)
    return jnp.clip(drawn, -reach, reach).astype(held_as)


def setup_inputs(seed: int = 0) -> dict:
    keys = jax.random.split(jax.random.key(seed), 8)
    return {
        "slice_starts": normal_values(keys[0], (SLICES, DOFS, ELEMS), 0.7, 3.0, ((0, 8), (2, 32)), jnp.float32),
        "window_entry": normal_values(keys[1], (DOFS, ELEMS), 0.7, 3.0, ((1, 32),), jnp.float32),
        "cell_order": jax.vmap(lambda own: jax.random.permutation(own, E_DEV))(jax.random.split(keys[2], PARTS_SIZE)).reshape((PARTS_SIZE, E_DEV)).astype(jnp.int32),
        "coarse_counts": plant(jax.random.randint(keys[3], (SLICES,), 1, 5), jax.random.fold_in(keys[3], 1), 1, 4).astype(jnp.int32),
        "advection_matrix": normal_values(keys[4], (DOFS, DOFS), DOFS ** -0.5, 0.75, (), jnp.float32),
        "viscous_matrix": normal_values(keys[5], (DOFS, DOFS), DOFS ** -0.5, 0.75, (), jnp.float32),
        "lift_matrix": normal_values(keys[6], (DOFS, 6 * FACE_DOFS), (6 * FACE_DOFS) ** -0.5, 0.625, (), jnp.float32),
    }


penalty = 0.5
time_step = 0.2
coarse_step = 0.1
coarse_visc = 0.5
face_signs = (-1.0, 1.0, -1.0, 1.0, -1.0, 1.0)


def face_traces(fields):
    columns = fields.shape[1]
    nodal_cube = fields.reshape(NODES, NODES, NODES, columns)
    top_node = NODES - 1
    face_slabs = (nodal_cube[0], nodal_cube[top_node], nodal_cube[:, 0], nodal_cube[:, top_node], nodal_cube[:, :, 0], nodal_cube[:, :, top_node])
    return [face_slab.reshape(NODES * NODES, columns) for face_slab in face_slabs]


def geometry(cell_order):
    cells_total = cell_order.shape[0]
    plane_size = LY * LZ
    layers = cells_total // plane_size
    slot_of_cell = jnp.zeros((cells_total,), jnp.int32).at[cell_order].set(jnp.arange(cells_total, dtype=jnp.int32))
    xcoord = cell_order // plane_size
    ycoord = (cell_order // LZ) % LY
    zcoord = cell_order % LZ
    in_plane = cell_order % plane_size

    def slot_at(x_pos, y_pos, z_pos):
        return slot_of_cell[(x_pos * LY + y_pos) * LZ + z_pos]

    x_below = jnp.where(xcoord > 0, slot_at(jnp.maximum(xcoord - 1, 0), ycoord, zcoord), cells_total + in_plane)
    x_above = jnp.where(xcoord < layers - 1, slot_at(jnp.minimum(xcoord + 1, layers - 1), ycoord, zcoord), cells_total + in_plane)
    y_below = slot_at(xcoord, (ycoord + LY - 1) % LY, zcoord)
    y_above = slot_at(xcoord, (ycoord + 1) % LY, zcoord)
    z_below = slot_at(xcoord, ycoord, (zcoord + LZ - 1) % LZ)
    z_above = slot_at(xcoord, ycoord, (zcoord + 1) % LZ)
    plane_index = jnp.arange(plane_size, dtype=jnp.int32)
    low_plane = slot_of_cell[plane_index]
    high_plane = slot_of_cell[(layers - 1) * plane_size + plane_index]
    return (x_below, x_above, y_below, y_above, z_below, z_above), low_plane, high_plane


def finish(fields, traces, ghost_below, ghost_above, neighbours, matrices):
    advection_matrix, viscous_matrix, lift_matrix = matrices
    sources = (jnp.concatenate([traces[1], ghost_below], axis=1), jnp.concatenate([traces[0], ghost_above], axis=1), traces[3], traces[2], traces[5], traces[4])
    face_terms = []
    for face_index in range(6):
        inside = traces[face_index]
        outside = jnp.take(sources[face_index], neighbours[face_index], axis=1)
        wave_speed = jnp.maximum(jnp.abs(inside), jnp.abs(outside))
        face_terms.append(0.25 * face_signs[face_index] * (inside * inside - outside * outside) + (0.5 * wave_speed + penalty) * (outside - inside))
    stacked = jnp.concatenate(face_terms, axis=0)
    highest = lax.Precision.HIGHEST
    volume = jnp.dot(advection_matrix, 0.5 * fields * fields, precision=highest, preferred_element_type=jnp.float32)
    viscous = jnp.dot(viscous_matrix, fields, precision=highest, preferred_element_type=jnp.float32)
    lifted = jnp.dot(lift_matrix, stacked, precision=highest, preferred_element_type=jnp.float32)
    return viscous - volume + lifted


def pick_columns(table, columns):
    return table[:, columns]


def tendency_all(fields, geoms, matrices):
    neighbours, low_planes, high_planes = geoms
    parts = low_planes.shape[0]
    blocks = fields.reshape(DOFS, parts, -1).transpose(1, 0, 2)
    traces = jax.vmap(face_traces)(blocks)
    lows = jax.vmap(pick_columns)(traces[0], low_planes)
    highs = jax.vmap(pick_columns)(traces[1], high_planes)
    ghost_below = jnp.roll(highs, 1, axis=0)
    ghost_above = jnp.roll(lows, -1, axis=0)
    result = jax.vmap(finish, in_axes=(0, 0, 0, 0, 0, None))(blocks, traces, ghost_below, ghost_above, neighbours, matrices)
    return result.transpose(1, 0, 2).reshape(DOFS, -1)


def reference(slice_starts, window_entry, cell_order, coarse_counts, advection_matrix, viscous_matrix, lift_matrix):
    matrices = (advection_matrix, viscous_matrix, lift_matrix)
    geoms = jax.vmap(geometry)(cell_order)

    def advance(fields):
        slope_one = tendency_all(fields, geoms, matrices)
        midpoint = fields + time_step * slope_one
        slope_two = tendency_all(midpoint, geoms, matrices)
        return fields + 0.5 * time_step * (slope_one + slope_two)

    def relax(fields):
        for repeat in range(STEPS - 1):
            fields = advance(fields)
        return fields

    own_ends = []
    for slice_index in range(SLICES):
        own_ends.append(advance(relax(slice_starts[slice_index])))
    correction = jnp.zeros((slice_starts.shape[2],), jnp.float32)
    starts_out = []
    interiors_out = []
    for slice_index in range(SLICES):
        relaxed = window_entry if slice_index == 0 else own_ends[slice_index - 1]
        corrected = relaxed + correction[None, :]
        starts_out.append(corrected)
        interiors_out.append(relax(corrected))
        if slice_index + 1 < SLICES:
            coarse_rhs = jnp.mean(advance(relax(relaxed)) - own_ends[slice_index], axis=0)
            steps_taken = coarse_counts[slice_index].astype(jnp.float32)
            factor = jnp.power(1.0 + coarse_step * (coarse_visc + jnp.abs(jnp.mean(relaxed, axis=0))), -steps_taken)
            correction = factor * correction + coarse_rhs
    return jnp.stack(starts_out), jnp.stack(interiors_out)
```

```python
import functools

import jax
import jax.numpy as jnp
from jax import lax
from jax.experimental import pallas as pl
from jax.experimental.pallas import tpu as pltpu
from jax.sharding import PartitionSpec as P

F32 = jnp.float32
BF16 = jnp.bfloat16
MESH = pl.DeviceIdType.MESH

DOFS = 64
EXT = 128
CELLS = 1024
LZ = 32
LANES = 128
BLOCKS = CELLS // LANES
CHUNKS = 4
WIDTH = CELLS // CHUNKS

PENALTY = 0.5
TIME_STEP = 0.2
COARSE_STEP = 0.1
COARSE_VISC = 0.5
HALF = 4
TOTAL = 10


def split2(v):
    high = v.astype(BF16)
    return high, (v - high.astype(F32)).astype(BF16)


def split3(v):
    high = v.astype(BF16)
    rest = v - high.astype(F32)
    middle = rest.astype(BF16)
    return high, middle, (rest - middle.astype(F32)).astype(BF16)


def flux(a, b):
    central = 0.25 * (a * a - b * b)
    speed = jnp.maximum(jnp.abs(a), jnp.abs(b))
    upwind = (0.5 * speed + PENALTY) * (b - a)
    return central, upwind


def expand_rows(ref):
    for i in range(4):
        ref[64 + 4 * i : 68 + 4 * i, :] = ref[16 * i : 16 * i + 4, :]
        ref[80 + 4 * i : 84 + 4 * i, :] = ref[16 * i + 12 : 16 * i + 16, :]
    for n in range(16):
        ref[96 + n : 97 + n, :] = ref[4 * n : 4 * n + 1, :]
        ref[112 + n : 113 + n, :] = ref[4 * n + 3 : 4 * n + 4, :]


def expand_weights(w):
    groups = [w]
    groups += [w[16 * i : 16 * i + 4] for i in range(4)]
    groups += [w[16 * i + 12 : 16 * i + 16] for i in range(4)]
    groups += [w[4 * n : 4 * n + 1] for n in range(16)]
    groups += [w[4 * n + 3 : 4 * n + 4] for n in range(16)]
    return jnp.concatenate(groups, axis=0)


def kernel(
    tm_count,
    space_count,
    start_hbm,
    entry_hbm,
    cell_ref,
    count_ref,
    adv_ref,
    visc_ref,
    lift_ref,
    starts_out,
    interiors_out,
    load,
    entry,
    onehot,
    pieces,
    state,
    base,
    partial,
    rhs_high,
    rhs_low,
    weights,
    weights_x,
    ghost,
    relaxed,
    own_end,
    early,
    late,
    corr,
    out_a,
    out_b,
    load_sem,
    ghost_send,
    ghost_recv,
    early_send,
    early_recv,
    late_send,
    late_recv,
    cross_send,
    cross_recv,
    out_sem,
):
    tm = lax.axis_index("tm")
    sp = lax.axis_index("space")
    above = lax.rem(sp + 1, space_count)
    below = lax.rem(sp + space_count - 1, space_count)
    last = tm_count - 1

    barrier = pltpu.get_barrier_semaphore()
    for other in (below, above):
        pl.semaphore_signal(barrier, inc=1, device_id=(tm, other), device_id_type=MESH)
    for d in range(1, tm_count):
        pl.semaphore_signal(
            barrier, inc=1, device_id=(lax.rem(tm + d, tm_count), sp), device_id_type=MESH
        )

    @pl.when(tm == last)
    def _():
        pltpu.make_async_copy(entry_hbm, load, load_sem.at[0]).start()

    @pl.when(tm != last)
    def _():
        pltpu.make_async_copy(start_hbm, load, load_sem.at[0]).start()

    @pl.when(tm == 0)
    def _():
        pltpu.make_async_copy(entry_hbm, entry, load_sem.at[1]).start()

    cell = cell_ref[...]
    in_y = cell >> 5
    in_z = cell & 31
    z_row = lax.broadcasted_iota(jnp.int32, (LZ, CELLS), 0)
    z_hot = jnp.where(z_row == in_z, 1.0, 0.0).astype(BF16)

    def build(y, _):
        hot = jnp.where(in_y == y, 1.0, 0.0)
        onehot[pl.ds(pl.multiple_of(y * LZ, LZ), LZ), :] = z_hot * jnp.broadcast_to(
            hot, (LZ, CELLS)
        ).astype(BF16)
        return 0

    lax.fori_loop(0, 32, build, 0)

    lift = lift_ref[...]
    main = jnp.concatenate([visc_ref[...], -adv_ref[...], lift[:, 32:96]], axis=1)
    main_high, main_low = split2(expand_weights(main))
    weights[0:EXT, :] = main_high
    weights[EXT : 2 * EXT, :] = main_low
    x_high, x_low = split2(expand_weights(lift[:, 0:32]))
    weights_x[...] = jnp.concatenate([x_high, x_low, x_high], axis=1)

    def to_lattice(source, target):
        high, middle, low = split3(source[...])
        pieces[0:64, :] = high
        pieces[64:128, :] = middle
        pieces[128:192, :] = low
        for t in range(4):
            lanes = slice(t * 256, (t + 1) * 256)
            found = lax.dot_general(
                pieces[...],
                onehot[lanes, :],
                (((1,), (1,)), ((), ())),
                preferred_element_type=F32,
            )
            target[0:64, lanes] = (found[0:64] + found[64:128]) + found[128:192]

    def to_slots(source, target):
        high, middle, low = split3(source[0:64, :])
        pieces[0:64, :] = high
        pieces[64:128, :] = middle
        pieces[128:192, :] = low
        for t in range(4):
            lanes = slice(t * 256, (t + 1) * 256)
            found = jnp.dot(pieces[...], onehot[:, lanes], preferred_element_type=F32)
            target[:, lanes] = (found[0:64] + found[64:128]) + found[128:192]

    def node_means(source, target, row):
        for b in range(BLOCKS):
            lanes = slice(b * LANES, (b + 1) * LANES)
            total = jnp.sum(source[0:64, lanes], axis=0, keepdims=True)
            target[row + b : row + b + 1, :] = total * (1.0 / DOFS)

    def ghost_copy(slot, side, c):
        lanes = pl.ds(c * WIDTH, WIDTH)
        rows = pl.ds(0, 16) if side == 1 else pl.ds(48, 16)
        return pltpu.make_async_remote_copy(
            src_ref=state.at[slot, rows, lanes],
            dst_ref=ghost.at[slot, side, :, lanes],
            send_sem=ghost_send.at[slot, side, c],
            recv_sem=ghost_recv.at[slot, side, c],
            device_id=(tm, below if side == 1 else above),
            device_id_type=MESH,
        )

    pltpu.make_async_copy(start_hbm, load, load_sem.at[0]).wait()
    first = state.at[0]
    to_lattice(load, first)
    expand_rows(first)
    base[...] = first[...]

    pl.semaphore_wait(barrier, 2 + tm_count - 1)
    for c in range(CHUNKS):
        for side in (0, 1):
            ghost_copy(0, side, c).start()

    mine = early.at[tm]
    node_means(first, mine, 16)
    mine[8:16, :] = jnp.full((8, LANES), count_ref[0].astype(F32))

    @pl.when(tm == 0)
    def _():
        pltpu.make_async_copy(entry_hbm, entry, load_sem.at[1]).wait()
        to_lattice(entry, relaxed)

    lane = lax.broadcasted_iota(jnp.int32, (16, LANES), 1)
    in_cell_z = lane & 31
    z_first = in_cell_z == 0
    z_last = in_cell_z == 31

    def early_copy(d):
        return pltpu.make_async_remote_copy(
            src_ref=early.at[tm],
            dst_ref=early.at[tm],
            send_sem=early_send.at[d - 1],
            recv_sem=early_recv.at[tm],
            device_id=(lax.rem(tm + d, tm_count), sp),
            device_id_type=MESH,
        )

    def early_arrival(d):
        source = lax.rem(tm + d, tm_count)
        return pltpu.make_async_remote_copy(
            src_ref=early.at[source],
            dst_ref=early.at[source],
            send_sem=early_send.at[d - 1],
            recv_sem=early_recv.at[source],
            device_id=(source, sp),
            device_id_type=MESH,
        )

    def late_copy(d):
        return pltpu.make_async_remote_copy(
            src_ref=late.at[tm],
            dst_ref=late.at[tm],
            send_sem=late_send.at[d - 1],
            recv_sem=late_recv.at[tm],
            device_id=(lax.rem(tm + d, tm_count), sp),
            device_id_type=MESH,
        )

    def late_arrival(d):
        source = lax.rem(tm + d, tm_count)
        return pltpu.make_async_remote_copy(
            src_ref=late.at[source],
            dst_ref=late.at[source],
            send_sem=late_send.at[d - 1],
            recv_sem=late_recv.at[source],
            device_id=(source, sp),
            device_id_type=MESH,
        )

    cross = pltpu.make_async_remote_copy(
        src_ref=own_end,
        dst_ref=relaxed.at[0:64, :],
        send_sem=cross_send,
        recv_sem=cross_recv,
        device_id=(lax.rem(tm + 1, tm_count), sp),
        device_id_type=MESH,
    )

    def step(it, _):
        slot = lax.rem(it, 2)
        other = 1 - slot
        now = state.at[slot]
        new = state.at[other]

        def put(row, lanes, value):
            high, low = split2(value)
            rhs_high[row : row + value.shape[0], lanes] = high
            rhs_low[row : row + value.shape[0], lanes] = low

        block = [slice(b * LANES, (b + 1) * LANES) for b in range(BLOCKS)]
        y_shift = [pltpu.roll(now[64:80, block[b]], LANES - LZ, 1) for b in range(BLOCKS)]
        back = []
        for b in range(BLOCKS):
            y_above = jnp.where(lane < LANES - LZ, y_shift[b], y_shift[(b + 1) % BLOCKS])
            central, upwind = flux(now[80:96, block[b]], y_above)
            put(144, block[b], central + upwind)
            back.append(pltpu.roll(central - upwind, LZ, 1))
        for b in range(BLOCKS):
            put(128, block[b], jnp.where(lane >= LZ, back[b], back[b - 1]))
        for b in range(BLOCKS):
            z_low = now[96:112, block[b]]
            z_above = jnp.where(
                z_last, pltpu.roll(z_low, 31, 1), pltpu.roll(z_low, LANES - 1, 1)
            )
            central, upwind = flux(now[112:128, block[b]], z_above)
            put(176, block[b], central + upwind)
            down = central - upwind
            put(
                160,
                block[b],
                jnp.where(z_first, pltpu.roll(down, LANES - 31, 1), pltpu.roll(down, 1, 1)),
            )
            values = now[0:64, block[b]]
            put(0, block[b], values)
            put(64, block[b], 0.5 * values * values)
        for t in range(4):
            lanes = slice(t * 256, (t + 1) * 256)
            both = jnp.dot(weights[...], rhs_high[:, lanes], preferred_element_type=F32)
            rest = jnp.dot(weights[0:EXT, :], rhs_low[:, lanes], preferred_element_type=F32)
            partial[:, lanes] = both[0:EXT] + (both[EXT : 2 * EXT] + rest)

        factor = jnp.where(slot == 0, TIME_STEP, 0.5 * TIME_STEP).astype(F32)
        @pl.when(it > 0)
        def _():
            for c in range(CHUNKS):
                for side in (0, 1):
                    ghost_copy(other, side, c).wait_send()

        for c in range(CHUNKS):
            lanes = slice(c * WIDTH, (c + 1) * WIDTH)
            for side in (0, 1):
                ghost_copy(slot, side, c).wait_recv()
            central, upwind = flux(ghost[slot, 0, :, lanes], now[0:16, lanes])
            low_term = central - upwind
            central, upwind = flux(now[48:64, lanes], ghost[slot, 1, :, lanes])
            term = jnp.concatenate([low_term, central + upwind], axis=0)
            high, low = split2(term)
            found = jnp.dot(
                weights_x[...],
                jnp.concatenate([high, high, low], axis=0),
                preferred_element_type=F32,
            )
            slope = partial[:, lanes] + found
            before = base[:, lanes]
            new[:, lanes] = before + factor * slope
            base[:, lanes] = before + (0.5 * TIME_STEP) * slope

            @pl.when(jnp.logical_and(it != 7, it != 9))
            def _():
                for side in (0, 1):
                    ghost_copy(other, side, c).start()

        @pl.when(it == HALF - 1)
        def _():
            own_end[...] = new[0:64, :]

            @pl.when(tm < last)
            def _():
                cross.start()

            node_means(new, early.at[tm], 0)
            for d in range(1, tm_count):
                early_copy(d).start()

        @pl.when(it == 2 * HALF - 1)
        def _():
            node_means(new, late.at[tm], 0)
            for d in range(1, tm_count):
                late_copy(d).start()
            for d in range(1, tm_count):
                early_arrival(d).wait_recv()

            @pl.when(tm > 0)
            def _():
                cross.wait_recv()

            expand_rows(relaxed)
            factors = []
            for j in range(tm_count - 1):
                mean = early[last, 16:24, :] if j == 0 else early[j - 1, 0:8, :]
                growth = jnp.log(1.0 + COARSE_STEP * (COARSE_VISC + jnp.abs(mean)))
                factors.append(jnp.exp(-early[j, 8:16, :] * growth))
            for d in range(1, tm_count):
                late_arrival(d).wait_recv()
            total = jnp.zeros((8, LANES), F32)
            for j in range(tm_count - 1):
                ended = early[last, 0:8, :] if j == 0 else late[j - 1]
                following = factors[j] * total + (ended - early[j, 0:8, :])
                total = jnp.where(tm > j, following, total)
            corr[...] = total
            for b in range(BLOCKS):
                lanes = slice(b * LANES, (b + 1) * LANES)
                value = relaxed[:, lanes] + corr[b : b + 1, :]
                new[:, lanes] = value
                base[:, lanes] = value
            for c in range(CHUNKS):
                for side in (0, 1):
                    ghost_copy(other, side, c).start()
            to_slots(base, out_a)
            pltpu.make_async_copy(out_a, starts_out, out_sem.at[0]).start()

        return 0

    lax.fori_loop(0, TOTAL, step, 0)

    to_slots(state.at[0], out_b)
    result = pltpu.make_async_copy(out_b, interiors_out, out_sem.at[1])
    result.start()
    for c in range(CHUNKS):
        for side in (0, 1):
            ghost_copy(1, side, c).wait_send()
    for d in range(1, tm_count):
        early_copy(d).wait_send()
        late_copy(d).wait_send()

    @pl.when(tm < last)
    def _():
        cross.wait_send()

    pltpu.make_async_copy(out_a, starts_out, out_sem.at[0]).wait()
    result.wait()


def body(tm_count, space_count, slice_starts, window_entry, cell_order, coarse_counts, adv, visc, lift):
    vmem = pl.BlockSpec(memory_space=pltpu.VMEM)
    anywhere = pl.BlockSpec(memory_space=pl.ANY)
    field = jax.ShapeDtypeStruct((DOFS, CELLS), F32)
    dma = pltpu.SemaphoreType.DMA
    starts, interiors = pl.pallas_call(
        functools.partial(kernel, tm_count, space_count),
        out_shape=(field, field),
        in_specs=[
            anywhere,
            anywhere,
            vmem,
            pl.BlockSpec(memory_space=pltpu.SMEM),
            vmem,
            vmem,
            vmem,
        ],
        out_specs=(anywhere, anywhere),
        scratch_shapes=[
            pltpu.VMEM((DOFS, CELLS), F32),
            pltpu.VMEM((DOFS, CELLS), F32),
            pltpu.VMEM((CELLS, CELLS), BF16),
            pltpu.VMEM((3 * DOFS, CELLS), BF16),
            pltpu.VMEM((2, EXT, CELLS), F32),
            pltpu.VMEM((EXT, CELLS), F32),
            pltpu.VMEM((EXT, CELLS), F32),
            pltpu.VMEM((192, CELLS), BF16),
            pltpu.VMEM((192, CELLS), BF16),
            pltpu.VMEM((2 * EXT, 192), BF16),
            pltpu.VMEM((EXT, 96), BF16),
            pltpu.VMEM((2, 2, 16, CELLS), F32),
            pltpu.VMEM((EXT, CELLS), F32),
            pltpu.VMEM((DOFS, CELLS), F32),
            pltpu.VMEM((tm_count, 24, LANES), F32),
            pltpu.VMEM((tm_count, 8, LANES), F32),
            pltpu.VMEM((8, LANES), F32),
            pltpu.VMEM((DOFS, CELLS), F32),
            pltpu.VMEM((DOFS, CELLS), F32),
            dma((2,)),
            dma((2, 2, CHUNKS)),
            dma((2, 2, CHUNKS)),
            dma((tm_count - 1,)),
            dma((tm_count,)),
            dma((tm_count - 1,)),
            dma((tm_count,)),
            dma,
            dma,
            dma((2,)),
        ],
        compiler_params=pltpu.CompilerParams(collective_id=0, has_side_effects=True),
        name="mgrit",
    )(slice_starts[0], window_entry, cell_order, coarse_counts, adv, visc, lift)
    return starts[None], interiors[None]


def solution(mesh):
    return jax.shard_map(
        functools.partial(body, mesh.shape["tm"], mesh.shape["space"]),
        mesh=mesh,
        in_specs=(
            P("tm", None, "space"),
            P(None, "space"),
            P("space", None),
            P("tm"),
            P(),
            P(),
            P(),
        ),
        out_specs=(P("tm", None, "space"), P("tm", None, "space")),
        check_vma=False,
    )
```

```python
import functools

import jax
import jax.numpy as jnp
from jax import lax
from jax.experimental import pallas as pl
from jax.experimental.pallas import tpu as pltpu
from jax.sharding import PartitionSpec as P

F32 = jnp.float32
BF16 = jnp.bfloat16
MESH = pl.DeviceIdType.MESH

DOFS = 64
EXT = 128
CELLS = 1024
LZ = 32
LANES = 128
BLOCKS = CELLS // LANES
CHUNKS = 4
WIDTH = CELLS // CHUNKS

PENALTY = 0.5
TIME_STEP = 0.2
COARSE_STEP = 0.1
COARSE_VISC = 0.5
HALF = 4


def split2(v):
    high = v.astype(BF16)
    return high, (v - high.astype(F32)).astype(BF16)


def split3(v):
    high = v.astype(BF16)
    rest = v - high.astype(F32)
    middle = rest.astype(BF16)
    return high, middle, (rest - middle.astype(F32)).astype(BF16)


def flux(a, b):
    central = 0.25 * (a * a - b * b)
    speed = jnp.maximum(jnp.abs(a), jnp.abs(b))
    upwind = (0.5 * speed + PENALTY) * (b - a)
    return central, upwind


def expand_rows(ref):
    for i in range(4):
        ref[64 + 4 * i : 68 + 4 * i, :] = ref[16 * i : 16 * i + 4, :]
        ref[80 + 4 * i : 84 + 4 * i, :] = ref[16 * i + 12 : 16 * i + 16, :]
    for n in range(16):
        ref[96 + n : 97 + n, :] = ref[4 * n : 4 * n + 1, :]
        ref[112 + n : 113 + n, :] = ref[4 * n + 3 : 4 * n + 4, :]


def expand_weights(w):
    groups = [w]
    groups += [w[16 * i : 16 * i + 4] for i in range(4)]
    groups += [w[16 * i + 12 : 16 * i + 16] for i in range(4)]
    groups += [w[4 * n : 4 * n + 1] for n in range(16)]
    groups += [w[4 * n + 3 : 4 * n + 4] for n in range(16)]
    return jnp.concatenate(groups, axis=0)


def kernel(
    tm_count,
    space_count,
    start_hbm,
    entry_hbm,
    cell_ref,
    count_ref,
    adv_ref,
    visc_ref,
    lift_ref,
    starts_out,
    interiors_out,
    load,
    entry,
    onehot,
    pieces,
    mine,
    twin,
    base,
    partial,
    rhs_high,
    rhs_low,
    weights,
    weights_x,
    ghost,
    final,
    last_ghost,
    relaxed,
    own_end,
    early,
    late,
    corr,
    out_a,
    out_b,
    load_sem,
    ghost_send,
    ghost_recv,
    field_send,
    field_recv,
    last_send,
    last_recv,
    early_send,
    early_recv,
    late_send,
    late_recv,
    cross_send,
    cross_recv,
    out_sem,
):
    tm = lax.axis_index("tm")
    sp = lax.axis_index("space")
    above = lax.rem(sp + 1, space_count)
    below = lax.rem(sp + space_count - 1, space_count)
    last = tm_count - 1

    barrier = pltpu.get_barrier_semaphore()
    two_above = lax.rem(sp + 2, space_count)
    two_below = lax.rem(sp + space_count - 2, space_count)
    for other in (below, above, two_below, two_above):
        pl.semaphore_signal(barrier, inc=1, device_id=(tm, other), device_id_type=MESH)
    for d in range(1, tm_count):
        pl.semaphore_signal(
            barrier, inc=1, device_id=(lax.rem(tm + d, tm_count), sp), device_id_type=MESH
        )

    @pl.when(tm == last)
    def _():
        pltpu.make_async_copy(entry_hbm, load, load_sem.at[0]).start()

    @pl.when(tm != last)
    def _():
        pltpu.make_async_copy(start_hbm, load, load_sem.at[0]).start()

    @pl.when(tm == 0)
    def _():
        pltpu.make_async_copy(entry_hbm, entry, load_sem.at[1]).start()

    cell = cell_ref[...]
    in_y = cell >> 5
    in_z = cell & 31
    z_row = lax.broadcasted_iota(jnp.int32, (LZ, CELLS), 0)
    z_hot = jnp.where(z_row == in_z, 1.0, 0.0).astype(BF16)

    def build(y, _):
        hot = jnp.where(in_y == y, 1.0, 0.0)
        onehot[pl.ds(pl.multiple_of(y * LZ, LZ), LZ), :] = z_hot * jnp.broadcast_to(
            hot, (LZ, CELLS)
        ).astype(BF16)
        return 0

    lax.fori_loop(0, 32, build, 0)

    lift = lift_ref[...]
    main = jnp.concatenate([visc_ref[...], -adv_ref[...], lift[:, 32:96]], axis=1)
    main_high, main_low = split2(expand_weights(main))
    weights[0:EXT, :] = main_high
    weights[EXT : 2 * EXT, :] = main_low
    x_high, x_low = split2(expand_weights(lift[:, 0:32]))
    weights_x[...] = jnp.concatenate([x_high, x_low, x_high], axis=1)

    def to_lattice(source, target):
        high, middle, low = split3(source[...])
        pieces[0:64, :] = high
        pieces[64:128, :] = middle
        pieces[128:192, :] = low
        for t in range(4):
            lanes = slice(t * 256, (t + 1) * 256)
            found = lax.dot_general(
                pieces[...],
                onehot[lanes, :],
                (((1,), (1,)), ((), ())),
                preferred_element_type=F32,
            )
            target[0:64, lanes] = (found[0:64] + found[64:128]) + found[128:192]

    def to_slots(source, target):
        high, middle, low = split3(source[0:64, :])
        pieces[0:64, :] = high
        pieces[64:128, :] = middle
        pieces[128:192, :] = low
        for t in range(4):
            lanes = slice(t * 256, (t + 1) * 256)
            found = jnp.dot(pieces[...], onehot[:, lanes], preferred_element_type=F32)
            target[:, lanes] = (found[0:64] + found[64:128]) + found[128:192]

    def node_means(source, target, row):
        for b in range(BLOCKS):
            lanes = slice(b * LANES, (b + 1) * LANES)
            total = jnp.sum(source[0:64, lanes], axis=0, keepdims=True)
            target[row + b : row + b + 1, :] = total * (1.0 / DOFS)

    odd = lax.rem(sp, 2)
    is_odd = odd == 1
    own = 1 - odd
    mate = sp + 1 - 2 * odd
    beyond = lax.rem(sp + 2 - 4 * odd + space_count, space_count)
    twin_device = lax.rem(sp - 1 + 2 * odd + space_count, space_count)
    out_rows = pl.multiple_of(48 * own, 16)
    near_rows = pl.multiple_of(48 * odd, 16)
    twin_rows = pl.multiple_of(48 * own, 16)
    rest_rows = pl.multiple_of(16 * own, 16)

    def trace_copy(slot, parity, which):
        return pltpu.make_async_remote_copy(
            src_ref=mine.at[parity, pl.ds(out_rows, 16), :],
            dst_ref=ghost.at[slot, odd],
            send_sem=ghost_send.at[parity, which],
            recv_sem=ghost_recv.at[slot, odd],
            device_id=(tm, beyond if which else mate),
            device_id_type=MESH,
        )

    def trace_wait(slot, side):
        pltpu.make_async_remote_copy(
            src_ref=mine.at[0, pl.ds(out_rows, 16), :],
            dst_ref=ghost.at[slot, side],
            send_sem=ghost_send.at[0, 0],
            recv_sem=ghost_recv.at[slot, side],
            device_id=(tm, mate),
            device_id_type=MESH,
        ).wait_recv()

    def field_copy(part):
        rows = pl.ds(near_rows, 16) if part == 0 else pl.ds(rest_rows, 48)
        return pltpu.make_async_remote_copy(
            src_ref=mine.at[0, rows, :],
            dst_ref=twin.at[0, rows, :],
            send_sem=field_send.at[part],
            recv_sem=field_recv.at[part],
            device_id=(tm, twin_device),
            device_id_type=MESH,
        )

    def field_wait(part):
        rows = pl.ds(twin_rows, 16) if part == 0 else pl.ds(pl.multiple_of(16 * odd, 16), 48)
        pltpu.make_async_remote_copy(
            src_ref=mine.at[0, rows, :],
            dst_ref=twin.at[0, rows, :],
            send_sem=field_send.at[part],
            recv_sem=field_recv.at[part],
            device_id=(tm, twin_device),
            device_id_type=MESH,
        ).wait_recv()

    def last_copy(slot, side, c):
        lanes = pl.ds(c * WIDTH, WIDTH)
        rows = pl.ds(0, 16) if side == 1 else pl.ds(48, 16)
        return pltpu.make_async_remote_copy(
            src_ref=final.at[slot, rows, lanes],
            dst_ref=last_ghost.at[slot, side, :, lanes],
            send_sem=last_send.at[slot, side, c],
            recv_sem=last_recv.at[slot, side, c],
            device_id=(tm, below if side == 1 else above),
            device_id_type=MESH,
        )

    lane = lax.broadcasted_iota(jnp.int32, (16, LANES), 1)
    in_cell_z = lane & 31
    z_first = in_cell_z == 0
    z_last = in_cell_z == 31

    def local_part(now, target):
        block = [slice(b * LANES, (b + 1) * LANES) for b in range(BLOCKS)]

        def put(row, lanes, value):
            high, low = split2(value)
            rhs_high[row : row + value.shape[0], lanes] = high
            rhs_low[row : row + value.shape[0], lanes] = low

        shifts = {}

        def y_shift(b):
            if b not in shifts:
                shifts[b] = pltpu.roll(now[64:80, block[b]], LANES - LZ, 1)
            return shifts[b]

        back = {}

        def y_high(b):
            if b not in back:
                y_above = jnp.where(lane < LANES - LZ, y_shift(b), y_shift((b + 1) % BLOCKS))
                central, upwind = flux(now[80:96, block[b]], y_above)
                put(144, block[b], central + upwind)
                back[b] = pltpu.roll(central - upwind, LZ, 1)
            return back[b]

        for t in range(4):
            for b in (2 * t, 2 * t + 1):
                before = y_high((b - 1) % BLOCKS)
                put(128, block[b], jnp.where(lane >= LZ, y_high(b), before))
                z_low = now[96:112, block[b]]
                z_above = jnp.where(
                    z_last, pltpu.roll(z_low, 31, 1), pltpu.roll(z_low, LANES - 1, 1)
                )
                central, upwind = flux(now[112:128, block[b]], z_above)
                put(176, block[b], central + upwind)
                down = central - upwind
                put(
                    160,
                    block[b],
                    jnp.where(z_first, pltpu.roll(down, LANES - 31, 1), pltpu.roll(down, 1, 1)),
                )
                values = now[0:64, block[b]]
                put(0, block[b], values)
                put(64, block[b], 0.5 * values * values)
            lanes = slice(t * 256, (t + 1) * 256)
            both = jnp.dot(weights[...], rhs_high[:, lanes], preferred_element_type=F32)
            rest = jnp.dot(weights[0:EXT, :], rhs_low[:, lanes], preferred_element_type=F32)
            target[:, lanes] = both[0:EXT] + (both[EXT : 2 * EXT] + rest)

    def x_part(stage, now, new, held, done, low_ghost, high_ghost, lanes):
        central, upwind = flux(low_ghost, now[0:16, lanes])
        low_term = central - upwind
        central, upwind = flux(now[48:64, lanes], high_ghost)
        high, low = split2(jnp.concatenate([low_term, central + upwind], axis=0))
        found = jnp.dot(
            weights_x[...],
            jnp.concatenate([high, high, low], axis=0),
            preferred_element_type=F32,
        )
        half = (0.5 * TIME_STEP) * (done[:, lanes] + found)
        if stage == 0:
            before = now[:, lanes]
            held[:, lanes] = before + half
            new[:, lanes] = before + (half + half)
        else:
            new[:, lanes] = held[:, lanes] + half

    tiles = [slice(c * 256, (c + 1) * 256) for c in range(4)]

    pltpu.make_async_copy(start_hbm, load, load_sem.at[0]).wait()
    first = mine.at[0]
    to_lattice(load, first)
    pl.semaphore_wait(barrier, 4 + tm_count - 1)
    trace_copy(0, 0, 0).start()
    field_copy(0).start()
    trace_copy(0, 0, 1).start()
    field_copy(1).start()

    expand_rows(first)
    local_part(first, partial.at[0])
    sent = early.at[tm]
    node_means(first, sent, 16)
    sent[8:16, :] = jnp.full((8, LANES), count_ref[0].astype(F32))

    @pl.when(tm == 0)
    def _():
        pltpu.make_async_copy(entry_hbm, entry, load_sem.at[1]).wait()
        to_lattice(entry, relaxed)


    def early_copy(d):
        return pltpu.make_async_remote_copy(
            src_ref=early.at[tm],
            dst_ref=early.at[tm],
            send_sem=early_send.at[d - 1],
            recv_sem=early_recv.at[tm],
            device_id=(lax.rem(tm + d, tm_count), sp),
            device_id_type=MESH,
        )

    def early_arrival(d):
        source = lax.rem(tm + d, tm_count)
        return pltpu.make_async_remote_copy(
            src_ref=early.at[source],
            dst_ref=early.at[source],
            send_sem=early_send.at[d - 1],
            recv_sem=early_recv.at[source],
            device_id=(source, sp),
            device_id_type=MESH,
        )

    def late_copy(d):
        return pltpu.make_async_remote_copy(
            src_ref=late.at[tm],
            dst_ref=late.at[tm],
            send_sem=late_send.at[d - 1],
            recv_sem=late_recv.at[tm],
            device_id=(lax.rem(tm + d, tm_count), sp),
            device_id_type=MESH,
        )

    def late_arrival(d):
        source = lax.rem(tm + d, tm_count)
        return pltpu.make_async_remote_copy(
            src_ref=late.at[source],
            dst_ref=late.at[source],
            send_sem=late_send.at[d - 1],
            recv_sem=late_recv.at[source],
            device_id=(source, sp),
            device_id_type=MESH,
        )

    cross = pltpu.make_async_remote_copy(
        src_ref=own_end,
        dst_ref=relaxed.at[0:64, :],
        send_sem=cross_send,
        recv_sem=cross_recv,
        device_id=(lax.rem(tm + 1, tm_count), sp),
        device_id_type=MESH,
    )

    def step(pair, _):
        for stage in (0, 1):
            slot = 2 * pair + stage
            next_slot = slot + 1
            mine_now, mine_new = mine.at[stage], mine.at[1 - stage]
            twin_now, twin_new = twin.at[stage], twin.at[1 - stage]

            def sent_before():
                trace_copy(0, 1 - stage, 0).wait_send()
                trace_copy(0, 1 - stage, 1).wait_send()

            if stage == 0:
                pl.when(pair > 0)(sent_before)

                @pl.when(pair == 0)
                def _():
                    field_wait(0)
            else:
                sent_before()

                @pl.when(pair == 0)
                def _():
                    for part in (0, 1):
                        field_copy(part).wait_send()

            trace_wait(slot, own)
            for lanes in tiles:
                came = ghost[slot, own, :, lanes]
                near = twin_now[pl.ds(twin_rows, 16), lanes]
                low_ghost = jnp.where(is_odd, came, near)
                high_ghost = jnp.where(is_odd, near, came)
                x_part(stage, mine_now, mine_new, base.at[0], partial.at[0], low_ghost, high_ghost, lanes)

            def send():
                trace_copy(next_slot, 1 - stage, 0).start()
                trace_copy(next_slot, 1 - stage, 1).start()

            def rest():
                trace_wait(slot, odd)
                for lanes in tiles:
                    came = ghost[slot, odd, :, lanes]
                    near = mine_now[pl.ds(near_rows, 16), lanes]
                    low_ghost = jnp.where(is_odd, near, came)
                    high_ghost = jnp.where(is_odd, came, near)
                    x_part(stage, twin_now, twin_new, base.at[1], partial.at[1], low_ghost, high_ghost, lanes)
                local_part(mine_new, partial.at[0])
                local_part(twin_new, partial.at[1])

            if stage == 0:
                send()

                @pl.when(pair == 0)
                def _():
                    field_wait(1)
                    expand_rows(twin_now)
                    local_part(twin_now, partial.at[1])

                rest()
            else:
                pl.when(pair < HALF - 1)(send)

                @pl.when(pair == HALF // 2 - 1)
                def _():
                    own_end[...] = mine_new[0:64, :]

                    @pl.when(tm < last)
                    def _():
                        cross.start()

                    node_means(mine_new, early.at[tm], 0)
                    for d in range(1, tm_count):
                        early_copy(d).start()

                pl.when(pair < HALF - 1)(rest)

        return 0

    lax.fori_loop(0, HALF, step, 0)

    node_means(mine.at[0], late.at[tm], 0)
    for d in range(1, tm_count):
        late_copy(d).start()
    for d in range(1, tm_count):
        early_arrival(d).wait_recv()

    @pl.when(tm > 0)
    def _():
        cross.wait_recv()

    expand_rows(relaxed)
    factors = []
    for j in range(tm_count - 1):
        mean = early[last, 16:24, :] if j == 0 else early[j - 1, 0:8, :]
        growth = jnp.log(1.0 + COARSE_STEP * (COARSE_VISC + jnp.abs(mean)))
        factors.append(jnp.exp(-early[j, 8:16, :] * growth))
    for d in range(1, tm_count):
        late_arrival(d).wait_recv()
    total = jnp.zeros((8, LANES), F32)
    for j in range(tm_count - 1):
        ended = early[last, 0:8, :] if j == 0 else late[j - 1]
        following = factors[j] * total + (ended - early[j, 0:8, :])
        total = jnp.where(tm > j, following, total)
    corr[...] = total
    begun = final.at[0]
    for b in range(BLOCKS):
        lanes = slice(b * LANES, (b + 1) * LANES)
        begun[:, lanes] = relaxed[:, lanes] + corr[b : b + 1, :]
    for c in range(CHUNKS):
        for side in (0, 1):
            last_copy(0, side, c).start()
    local_part(begun, partial.at[0])
    to_slots(begun, out_a)
    first_result = pltpu.make_async_copy(out_a, starts_out, out_sem.at[0])
    first_result.start()

    for stage in (0, 1):
        for c in range(CHUNKS):
            for side in (0, 1):
                last_copy(stage, side, c).wait_recv()
            for k in range(WIDTH // 256):
                lanes = slice(c * WIDTH + k * 256, c * WIDTH + (k + 1) * 256)
                x_part(
                    stage,
                    final.at[stage],
                    final.at[stage + 1],
                    base.at[0],
                    partial.at[0],
                    last_ghost[stage, 0, :, lanes],
                    last_ghost[stage, 1, :, lanes],
                    lanes,
                )
            if stage == 0:
                for side in (0, 1):
                    last_copy(1, side, c).start()
        if stage == 0:
            local_part(final.at[1], partial.at[0])

    to_slots(final.at[2], out_b)
    result = pltpu.make_async_copy(out_b, interiors_out, out_sem.at[1])
    result.start()
    for c in range(CHUNKS):
        for slot in (0, 1):
            for side in (0, 1):
                last_copy(slot, side, c).wait_send()
    trace_wait(2 * HALF - 1, odd)
    for which in (0, 1):
        trace_copy(0, 1, which).wait_send()
    for d in range(1, tm_count):
        early_copy(d).wait_send()
        late_copy(d).wait_send()

    @pl.when(tm < last)
    def _():
        cross.wait_send()

    first_result.wait()
    result.wait()


def body(tm_count, space_count, slice_starts, window_entry, cell_order, coarse_counts, adv, visc, lift):
    vmem = pl.BlockSpec(memory_space=pltpu.VMEM)
    anywhere = pl.BlockSpec(memory_space=pl.ANY)
    field = jax.ShapeDtypeStruct((DOFS, CELLS), F32)
    dma = pltpu.SemaphoreType.DMA
    starts, interiors = pl.pallas_call(
        functools.partial(kernel, tm_count, space_count),
        out_shape=(field, field),
        in_specs=[
            anywhere,
            anywhere,
            vmem,
            pl.BlockSpec(memory_space=pltpu.SMEM),
            vmem,
            vmem,
            vmem,
        ],
        out_specs=(anywhere, anywhere),
        scratch_shapes=[
            pltpu.VMEM((DOFS, CELLS), F32),
            pltpu.VMEM((DOFS, CELLS), F32),
            pltpu.VMEM((CELLS, CELLS), BF16),
            pltpu.VMEM((3 * DOFS, CELLS), BF16),
            pltpu.VMEM((2, EXT, CELLS), F32),
            pltpu.VMEM((2, EXT, CELLS), F32),
            pltpu.VMEM((2, EXT, CELLS), F32),
            pltpu.VMEM((2, EXT, CELLS), F32),
            pltpu.VMEM((192, CELLS), BF16),
            pltpu.VMEM((192, CELLS), BF16),
            pltpu.VMEM((2 * EXT, 192), BF16),
            pltpu.VMEM((EXT, 96), BF16),
            pltpu.VMEM((2 * HALF, 2, 16, CELLS), F32),
            pltpu.VMEM((3, EXT, CELLS), F32),
            pltpu.VMEM((2, 2, 16, CELLS), F32),
            pltpu.VMEM((EXT, CELLS), F32),
            pltpu.VMEM((DOFS, CELLS), F32),
            pltpu.VMEM((tm_count, 24, LANES), F32),
            pltpu.VMEM((tm_count, 8, LANES), F32),
            pltpu.VMEM((8, LANES), F32),
            pltpu.VMEM((DOFS, CELLS), F32),
            pltpu.VMEM((DOFS, CELLS), F32),
            dma((2,)),
            dma((2, 2)),
            dma((2 * HALF, 2)),
            dma((2,)),
            dma((2,)),
            dma((2, 2, CHUNKS)),
            dma((2, 2, CHUNKS)),
            dma((tm_count - 1,)),
            dma((tm_count,)),
            dma((tm_count - 1,)),
            dma((tm_count,)),
            dma,
            dma,
            dma((2,)),
        ],
        compiler_params=pltpu.CompilerParams(collective_id=0, has_side_effects=True),
        name="mgrit",
    )(slice_starts[0], window_entry, cell_order, coarse_counts, adv, visc, lift)
    return starts[None], interiors[None]


def solution(mesh):
    return jax.shard_map(
        functools.partial(body, mesh.shape["tm"], mesh.shape["space"]),
        mesh=mesh,
        in_specs=(
            P("tm", None, "space"),
            P(None, "space"),
            P("space", None),
            P("tm"),
            P(),
            P(),
            P(),
        ),
        out_specs=(P("tm", None, "space"), P("tm", None, "space")),
        check_vma=False,
    )
```

```python
import functools

import jax
import jax.numpy as jnp
from jax import lax
from jax.experimental import pallas as pl
from jax.experimental.pallas import tpu as pltpu
from jax.sharding import PartitionSpec as P

F32 = jnp.float32
BF16 = jnp.bfloat16
MESH = pl.DeviceIdType.MESH

DOFS = 64
EXT = 128
CELLS = 1024
LZ = 32
LANES = 128
BLOCKS = CELLS // LANES
CHUNKS = 4
WIDTH = CELLS // CHUNKS

PENALTY = 0.5
TIME_STEP = 0.2
COARSE_STEP = 0.1
COARSE_VISC = 0.5
HALF = 4


def split2(v):
    high = v.astype(BF16)
    return high, (v - high.astype(F32)).astype(BF16)


def to_slots(source, pieces, onehot, target):
    high, low = split2(source[0:64, :])
    pieces[0:64, :] = high
    pieces[64:128, :] = low
    for t in range(4):
        lanes = slice(t * 256, (t + 1) * 256)
        found = jnp.dot(pieces[...], onehot[:, lanes], preferred_element_type=F32)
        target[:, lanes] = found[0:64] + found[64:128]


def flux(a, b):
    jump = b - a
    middle = 0.5 * (a + b)
    speed = jnp.maximum(jnp.abs(a), jnp.abs(b)) + 2.0 * PENALTY
    return jump * (speed - middle), jump * (speed + middle)


def expand_rows(ref):
    for i in range(4):
        ref[64 + 4 * i : 68 + 4 * i, :] = ref[16 * i : 16 * i + 4, :]
        ref[80 + 4 * i : 84 + 4 * i, :] = ref[16 * i + 12 : 16 * i + 16, :]
    for n in range(16):
        ref[96 + n : 97 + n, :] = ref[4 * n : 4 * n + 1, :]
        ref[112 + n : 113 + n, :] = ref[4 * n + 3 : 4 * n + 4, :]


def expand_weights(w):
    groups = [w]
    groups += [w[16 * i : 16 * i + 4] for i in range(4)]
    groups += [w[16 * i + 12 : 16 * i + 16] for i in range(4)]
    groups += [w[4 * n : 4 * n + 1] for n in range(16)]
    groups += [w[4 * n + 3 : 4 * n + 4] for n in range(16)]
    return jnp.concatenate(groups, axis=0)


def kernel(
    tm_count,
    space_count,
    start_hbm,
    entry_hbm,
    cell_hbm,
    count_ref,
    adv_hbm,
    visc_hbm,
    lift_hbm,
    starts_out,
    interiors_out,
    onehot,
    load,
    entry,
    cell_ref,
    adv_ref,
    visc_ref,
    lift_ref,
    pieces,
    mine,
    twin,
    base,
    partial,
    rhs,
    weights,
    weights_x,
    ghost,
    final,
    last_ghost,
    relaxed,
    own_end,
    early,
    late,
    corr,
    load_sem,
    ghost_send,
    ghost_recv,
    field_send,
    field_recv,
    last_send,
    last_recv,
    early_send,
    early_recv,
    late_send,
    late_recv,
    cross_send,
    cross_recv,
):
    tm = lax.axis_index("tm")
    sp = lax.axis_index("space")
    above = lax.rem(sp + 1, space_count)
    below = lax.rem(sp + space_count - 1, space_count)
    last = tm_count - 1

    small = [
        pltpu.make_async_copy(source, target, load_sem.at[2 + k])
        for k, (source, target) in enumerate(
            ((cell_hbm, cell_ref), (adv_hbm, adv_ref), (visc_hbm, visc_ref), (lift_hbm, lift_ref))
        )
    ]
    for copy in small:
        copy.start()

    @pl.when(tm == last)
    def _():
        pltpu.make_async_copy(entry_hbm, load, load_sem.at[0]).start()

    @pl.when(tm != last)
    def _():
        pltpu.make_async_copy(start_hbm, load, load_sem.at[0]).start()

    @pl.when(tm == 0)
    def _():
        pltpu.make_async_copy(entry_hbm, entry, load_sem.at[1]).start()

    barrier = pltpu.get_barrier_semaphore()
    two_above = lax.rem(sp + 2, space_count)
    two_below = lax.rem(sp + space_count - 2, space_count)
    for other in (below, above, two_below, two_above):
        pl.semaphore_signal(barrier, inc=1, device_id=(tm, other), device_id_type=MESH)
    for d in range(1, tm_count):
        pl.semaphore_signal(
            barrier, inc=1, device_id=(lax.rem(tm + d, tm_count), sp), device_id_type=MESH
        )

    small[0].wait()
    cell = cell_ref[...]
    in_y = cell >> 5
    in_z = cell & 31
    z_row = lax.broadcasted_iota(jnp.int32, (LZ, CELLS), 0)
    z_hot = jnp.where(z_row == in_z, 1.0, 0.0).astype(BF16)

    def build(y, _):
        hot = jnp.where(in_y == y, 1.0, 0.0)
        onehot[pl.ds(pl.multiple_of(y * LZ, LZ), LZ), :] = z_hot * jnp.broadcast_to(
            hot, (LZ, CELLS)
        ).astype(BF16)
        return 0

    lax.fori_loop(0, 32, build, 0, unroll=4)

    for copy in small[1:]:
        copy.wait()
    half_step = 0.5 * TIME_STEP
    side = (lax.broadcasted_iota(jnp.int32, (DOFS, 96), 1) >> 4) & 1
    lift = lift_ref[...] * jnp.where(side == 1, 0.5 * half_step, -0.5 * half_step)
    main = jnp.concatenate(
        [half_step * visc_ref[...], (-0.5 * half_step) * adv_ref[...], lift[:, 32:96]], axis=1
    )
    main_high, main_low = split2(expand_weights(main))
    weights[...] = jnp.concatenate([main_high, main_low, main_high], axis=1)
    x_high, x_low = split2(expand_weights(lift[:, 0:32]))
    weights_x[...] = jnp.concatenate([x_high, x_low, x_high], axis=1)

    def to_lattice(source, target):
        high, low = split2(source[...])
        pieces[0:64, :] = high
        pieces[64:128, :] = low
        for t in range(4):
            lanes = slice(t * 256, (t + 1) * 256)
            found = lax.dot_general(
                pieces[...],
                onehot[lanes, :],
                (((1,), (1,)), ((), ())),
                preferred_element_type=F32,
            )
            target[0:64, lanes] = found[0:64] + found[64:128]

    def node_means(source, target, row):
        for b in range(BLOCKS):
            lanes = slice(b * LANES, (b + 1) * LANES)
            total = jnp.sum(source[0:64, lanes], axis=0, keepdims=True)
            target[row + b : row + b + 1, :] = total * (1.0 / DOFS)

    odd = lax.rem(sp, 2)
    is_odd = odd == 1
    own = 1 - odd
    mate = sp + 1 - 2 * odd
    beyond = lax.rem(sp + 2 - 4 * odd + space_count, space_count)
    twin_device = lax.rem(sp - 1 + 2 * odd + space_count, space_count)
    out_rows = pl.multiple_of(48 * own, 16)
    near_rows = pl.multiple_of(48 * odd, 16)
    twin_rows = pl.multiple_of(48 * own, 16)
    rest_rows = pl.multiple_of(16 * own, 16)

    def trace_copy(slot, parity, which):
        return pltpu.make_async_remote_copy(
            src_ref=mine.at[parity, pl.ds(out_rows, 16), :],
            dst_ref=ghost.at[slot, odd],
            send_sem=ghost_send.at[parity, which],
            recv_sem=ghost_recv.at[slot, odd],
            device_id=(tm, beyond if which else mate),
            device_id_type=MESH,
        )

    def trace_wait(slot, side):
        pltpu.make_async_remote_copy(
            src_ref=mine.at[0, pl.ds(out_rows, 16), :],
            dst_ref=ghost.at[slot, side],
            send_sem=ghost_send.at[0, 0],
            recv_sem=ghost_recv.at[slot, side],
            device_id=(tm, mate),
            device_id_type=MESH,
        ).wait_recv()

    def field_copy(part):
        rows = pl.ds(near_rows, 16) if part == 0 else pl.ds(rest_rows, 48)
        return pltpu.make_async_remote_copy(
            src_ref=mine.at[0, rows, :],
            dst_ref=twin.at[0, rows, :],
            send_sem=field_send.at[part],
            recv_sem=field_recv.at[part],
            device_id=(tm, twin_device),
            device_id_type=MESH,
        )

    def field_wait(part):
        rows = pl.ds(twin_rows, 16) if part == 0 else pl.ds(pl.multiple_of(16 * odd, 16), 48)
        pltpu.make_async_remote_copy(
            src_ref=mine.at[0, rows, :],
            dst_ref=twin.at[0, rows, :],
            send_sem=field_send.at[part],
            recv_sem=field_recv.at[part],
            device_id=(tm, twin_device),
            device_id_type=MESH,
        ).wait_recv()

    def last_copy(slot, side, c):
        lanes = pl.ds(c * WIDTH, WIDTH)
        rows = pl.ds(0, 16) if side == 1 else pl.ds(48, 16)
        return pltpu.make_async_remote_copy(
            src_ref=final.at[slot, rows, lanes],
            dst_ref=last_ghost.at[slot, side, :, lanes],
            send_sem=last_send.at[slot, side, c],
            recv_sem=last_recv.at[slot, side, c],
            device_id=(tm, below if side == 1 else above),
            device_id_type=MESH,
        )

    lane = lax.broadcasted_iota(jnp.int32, (16, LANES), 1)
    in_cell_z = lane & 31
    z_first = in_cell_z == 0
    z_last = in_cell_z == 31

    def local_part(now, target):
        block = [slice(b * LANES, (b + 1) * LANES) for b in range(BLOCKS)]

        def put(row, lanes, value):
            high, low = split2(value)
            rhs[row : row + value.shape[0], lanes] = high
            rhs[192 + row : 192 + row + value.shape[0], lanes] = low

        shifts = {}

        def y_shift(b):
            if b not in shifts:
                shifts[b] = pltpu.roll(now[64:80, block[b]], LANES - LZ, 1)
            return shifts[b]

        back = {}

        def y_high(b):
            if b not in back:
                y_above = jnp.where(lane < LANES - LZ, y_shift(b), y_shift((b + 1) % BLOCKS))
                up, down = flux(now[80:96, block[b]], y_above)
                put(144, block[b], up)
                back[b] = pltpu.roll(down, LZ, 1)
            return back[b]

        for t in range(4):
            for b in (2 * t, 2 * t + 1):
                before = y_high((b - 1) % BLOCKS)
                put(128, block[b], jnp.where(lane >= LZ, y_high(b), before))
                z_low = now[96:112, block[b]]
                z_above = jnp.where(
                    z_last, pltpu.roll(z_low, 31, 1), pltpu.roll(z_low, LANES - 1, 1)
                )
                up, down = flux(now[112:128, block[b]], z_above)
                put(176, block[b], up)
                put(
                    160,
                    block[b],
                    jnp.where(z_first, pltpu.roll(down, LANES - 31, 1), pltpu.roll(down, 1, 1)),
                )
                values = now[0:64, block[b]]
                put(0, block[b], values)
                put(64, block[b], values * values)
            lanes = slice(t * 256, (t + 1) * 256)
            high = rhs[0:192, lanes]
            target[:, lanes] = jnp.dot(
                weights[...],
                jnp.concatenate([high, high, rhs[192:384, lanes]], axis=0),
                preferred_element_type=F32,
            )

    def x_part(stage, now, new, held, done, low_ghost, high_ghost, lanes):
        low_term = flux(low_ghost, now[0:16, lanes])[1]
        high_term = flux(now[48:64, lanes], high_ghost)[0]
        high, low = split2(jnp.concatenate([low_term, high_term], axis=0))
        found = jnp.dot(
            weights_x[...],
            jnp.concatenate([high, high, low], axis=0),
            preferred_element_type=F32,
        )
        half = done[:, lanes] + found
        if stage == 0:
            middle = now[:, lanes] + half
            held[:, lanes] = middle
            new[:, lanes] = middle + half
        else:
            new[:, lanes] = held[:, lanes] + half

    tiles = [slice(c * 256, (c + 1) * 256) for c in range(4)]

    pltpu.make_async_copy(start_hbm, load, load_sem.at[0]).wait()
    first = mine.at[0]
    to_lattice(load, first)
    pl.semaphore_wait(barrier, 4 + tm_count - 1)
    trace_copy(0, 0, 0).start()
    field_copy(0).start()
    trace_copy(0, 0, 1).start()
    field_copy(1).start()

    expand_rows(first)
    local_part(first, partial.at[0])
    sent = early.at[tm]
    node_means(first, sent, 16)
    sent[8:16, :] = jnp.full((8, LANES), count_ref[0].astype(F32))

    @pl.when(tm == 0)
    def _():
        pltpu.make_async_copy(entry_hbm, entry, load_sem.at[1]).wait()
        to_lattice(entry, relaxed)


    def early_copy(d):
        return pltpu.make_async_remote_copy(
            src_ref=early.at[tm],
            dst_ref=early.at[tm],
            send_sem=early_send.at[d - 1],
            recv_sem=early_recv.at[tm],
            device_id=(lax.rem(tm + d, tm_count), sp),
            device_id_type=MESH,
        )

    def early_arrival(d):
        source = lax.rem(tm + d, tm_count)
        return pltpu.make_async_remote_copy(
            src_ref=early.at[source],
            dst_ref=early.at[source],
            send_sem=early_send.at[d - 1],
            recv_sem=early_recv.at[source],
            device_id=(source, sp),
            device_id_type=MESH,
        )

    def late_copy(d):
        return pltpu.make_async_remote_copy(
            src_ref=late.at[tm],
            dst_ref=late.at[tm],
            send_sem=late_send.at[d - 1],
            recv_sem=late_recv.at[tm],
            device_id=(lax.rem(tm + d, tm_count), sp),
            device_id_type=MESH,
        )

    def late_arrival(d):
        source = lax.rem(tm + d, tm_count)
        return pltpu.make_async_remote_copy(
            src_ref=late.at[source],
            dst_ref=late.at[source],
            send_sem=late_send.at[d - 1],
            recv_sem=late_recv.at[source],
            device_id=(source, sp),
            device_id_type=MESH,
        )

    cross = pltpu.make_async_remote_copy(
        src_ref=own_end,
        dst_ref=relaxed.at[0:64, :],
        send_sem=cross_send,
        recv_sem=cross_recv,
        device_id=(lax.rem(tm + 1, tm_count), sp),
        device_id_type=MESH,
    )

    def step(pair, _):
        for stage in (0, 1):
            slot = 2 * pair + stage
            next_slot = slot + 1
            mine_now, mine_new = mine.at[stage], mine.at[1 - stage]
            twin_now, twin_new = twin.at[stage], twin.at[1 - stage]

            def sent_before():
                trace_copy(0, 1 - stage, 0).wait_send()
                trace_copy(0, 1 - stage, 1).wait_send()

            if stage == 0:
                pl.when(pair > 0)(sent_before)

                @pl.when(pair == 0)
                def _():
                    field_wait(0)
            else:
                sent_before()

                @pl.when(pair == 0)
                def _():
                    for part in (0, 1):
                        field_copy(part).wait_send()

            trace_wait(slot, own)
            for lanes in tiles:
                came = ghost[slot, own, :, lanes]
                near = twin_now[pl.ds(twin_rows, 16), lanes]
                low_ghost = jnp.where(is_odd, came, near)
                high_ghost = jnp.where(is_odd, near, came)
                x_part(stage, mine_now, mine_new, base.at[0], partial.at[0], low_ghost, high_ghost, lanes)

            def send():
                trace_copy(next_slot, 1 - stage, 0).start()
                trace_copy(next_slot, 1 - stage, 1).start()

            def rest():
                if stage == 0:

                    @pl.when(pair == 0)
                    def _():
                        field_wait(1)
                        expand_rows(twin_now)

                local_part(twin_now, partial.at[1])
                local_part(mine_new, partial.at[0])

                trace_wait(slot, odd)
                for lanes in tiles:
                    came = ghost[slot, odd, :, lanes]
                    near = mine_now[pl.ds(near_rows, 16), lanes]
                    low_ghost = jnp.where(is_odd, near, came)
                    high_ghost = jnp.where(is_odd, came, near)
                    x_part(stage, twin_now, twin_new, base.at[1], partial.at[1], low_ghost, high_ghost, lanes)

            if stage == 0:
                send()
                rest()
            else:
                pl.when(pair < HALF - 1)(send)

                @pl.when(pair == HALF // 2 - 1)
                def _():
                    own_end[...] = mine_new[0:64, :]

                    @pl.when(tm < last)
                    def _():
                        cross.start()

                    node_means(mine_new, early.at[tm], 0)
                    for d in range(1, tm_count):
                        early_copy(d).start()

                pl.when(pair < HALF - 1)(rest)

        return 0

    lax.fori_loop(0, HALF, step, 0)

    node_means(mine.at[0], late.at[tm], 0)
    for d in range(1, tm_count):
        late_copy(d).start()
    for d in range(1, tm_count):
        early_arrival(d).wait_recv()

    @pl.when(tm > 0)
    def _():
        cross.wait_recv()

    expand_rows(relaxed)
    factors = []
    for j in range(tm_count - 1):
        mean = early[last, 16:24, :] if j == 0 else early[j - 1, 0:8, :]
        growth = jnp.log(1.0 + COARSE_STEP * (COARSE_VISC + jnp.abs(mean)))
        factors.append(jnp.exp(-early[j, 8:16, :] * growth))
    for d in range(1, tm_count):
        late_arrival(d).wait_recv()
    total = jnp.zeros((8, LANES), F32)
    for j in range(tm_count - 1):
        ended = early[last, 0:8, :] if j == 0 else late[j - 1]
        following = factors[j] * total + (ended - early[j, 0:8, :])
        total = jnp.where(tm > j, following, total)
    corr[...] = total
    begun = final.at[0]
    for b in range(BLOCKS):
        lanes = slice(b * LANES, (b + 1) * LANES)
        begun[:, lanes] = relaxed[:, lanes] + corr[b : b + 1, :]
    for c in range(CHUNKS):
        for side in (0, 1):
            last_copy(0, side, c).start()
    local_part(begun, partial.at[0])
    to_slots(begun, pieces, onehot, starts_out)

    for stage in (0, 1):
        for c in range(CHUNKS):
            for side in (0, 1):
                last_copy(stage, side, c).wait_recv()
            for k in range(WIDTH // 256):
                lanes = slice(c * WIDTH + k * 256, c * WIDTH + (k + 1) * 256)
                x_part(
                    stage,
                    final.at[stage],
                    final.at[stage + 1],
                    base.at[0],
                    partial.at[0],
                    last_ghost[stage, 0, :, lanes],
                    last_ghost[stage, 1, :, lanes],
                    lanes,
                )
            if stage == 0:
                for side in (0, 1):
                    last_copy(1, side, c).start()
        if stage == 0:
            local_part(final.at[1], partial.at[0])

    interiors_out[...] = final[2, 0:64, :]
    for c in range(CHUNKS):
        for slot in (0, 1):
            for side in (0, 1):
                last_copy(slot, side, c).wait_send()
    trace_wait(2 * HALF - 1, odd)
    for which in (0, 1):
        trace_copy(0, 1, which).wait_send()
    for d in range(1, tm_count):
        early_copy(d).wait_send()
        late_copy(d).wait_send()

    @pl.when(tm < last)
    def _():
        cross.wait_send()


def deliver(starts, interiors, onehot, starts_out, interiors_out, pieces, placed, sem):
    first = pltpu.make_async_copy(starts, starts_out, sem.at[4])
    first.start()
    high, low = split2(interiors[...])
    pieces[0:64, :] = high
    pieces[64:128, :] = low
    copies = []
    for t in range(4):
        lanes = slice(t * 256, (t + 1) * 256)
        found = jnp.dot(pieces[...], onehot[:, lanes], preferred_element_type=F32)
        placed[:, lanes] = found[0:64] + found[64:128]
        copies.append(
            pltpu.make_async_copy(placed.at[:, lanes], interiors_out.at[:, lanes], sem.at[t])
        )
        copies[t].start()
    for copy in copies:
        copy.wait()
    first.wait()


def body(tm_count, space_count, slice_starts, window_entry, cell_order, coarse_counts, adv, visc, lift):
    vmem = pl.BlockSpec(memory_space=pltpu.VMEM)
    hbm = pl.BlockSpec(memory_space=pltpu.HBM)
    field = jax.ShapeDtypeStruct((DOFS, CELLS), F32)
    stay = functools.partial(pltpu.with_memory_space_constraint, memory_space=pltpu.HBM)
    dma = pltpu.SemaphoreType.DMA
    starts, interiors, onehot = pl.pallas_call(
        functools.partial(kernel, tm_count, space_count),
        out_shape=(field, field, jax.ShapeDtypeStruct((CELLS, CELLS), BF16)),
        in_specs=[
            hbm,
            hbm,
            hbm,
            pl.BlockSpec(memory_space=pltpu.SMEM),
            hbm,
            hbm,
            hbm,
        ],
        out_specs=(vmem, vmem, vmem),
        scratch_shapes=[
            pltpu.VMEM((DOFS, CELLS), F32),
            pltpu.VMEM((DOFS, CELLS), F32),
            pltpu.VMEM((1, CELLS), jnp.int32),
            pltpu.VMEM((DOFS, DOFS), F32),
            pltpu.VMEM((DOFS, DOFS), F32),
            pltpu.VMEM((DOFS, 96), F32),
            pltpu.VMEM((2 * DOFS, CELLS), BF16),
            pltpu.VMEM((2, EXT, CELLS), F32),
            pltpu.VMEM((2, EXT, CELLS), F32),
            pltpu.VMEM((2, EXT, CELLS), F32),
            pltpu.VMEM((2, EXT, CELLS), F32),
            pltpu.VMEM((384, CELLS), BF16),
            pltpu.VMEM((EXT, 576), BF16),
            pltpu.VMEM((EXT, 96), BF16),
            pltpu.VMEM((2 * HALF, 2, 16, CELLS), F32),
            pltpu.VMEM((3, EXT, CELLS), F32),
            pltpu.VMEM((2, 2, 16, CELLS), F32),
            pltpu.VMEM((EXT, CELLS), F32),
            pltpu.VMEM((DOFS, CELLS), F32),
            pltpu.VMEM((tm_count, 24, LANES), F32),
            pltpu.VMEM((tm_count, 8, LANES), F32),
            pltpu.VMEM((8, LANES), F32),
            dma((6,)),
            dma((2, 2)),
            dma((2 * HALF, 2)),
            dma((2,)),
            dma((2,)),
            dma((2, 2, CHUNKS)),
            dma((2, 2, CHUNKS)),
            dma((tm_count - 1,)),
            dma((tm_count,)),
            dma((tm_count - 1,)),
            dma((tm_count,)),
            dma,
            dma,
        ],
        compiler_params=pltpu.CompilerParams(
            collective_id=0, has_side_effects=True, vmem_limit_bytes=24 << 20
        ),
        name="mgrit",
    )(
        stay(slice_starts[0]),
        stay(window_entry),
        stay(cell_order),
        coarse_counts,
        stay(adv),
        stay(visc),
        stay(lift),
    )
    starts, interiors = pl.pallas_call(
        deliver,
        out_shape=(field, field),
        in_specs=[vmem, vmem, vmem],
        out_specs=(hbm, hbm),
        scratch_shapes=[
            pltpu.VMEM((2 * DOFS, CELLS), BF16),
            pltpu.VMEM((DOFS, CELLS), F32),
            dma((5,)),
        ],
        compiler_params=pltpu.CompilerParams(vmem_limit_bytes=24 << 20),
        name="deliver",
    )(starts, interiors, onehot)
    return starts[None], interiors[None]


def solution(mesh):
    return jax.shard_map(
        functools.partial(body, mesh.shape["tm"], mesh.shape["space"]),
        mesh=mesh,
        in_specs=(
            P("tm", None, "space"),
            P(None, "space"),
            P("space", None),
            P("tm"),
            P(),
            P(),
            P(),
        ),
        out_specs=(P("tm", None, "space"), P("tm", None, "space")),
        check_vma=False,
    )
```
